128 devices in a mesh: sector: 4 (over y_hi, core), owner: 32 (over x, y_lo, z).
Axes of the slice: x: 4, y: 4 (y_hi: 2, y_lo: 2; y = y_hi * 2 + y_lo), z: 4, core: 2. Of those that a mesh axis runs over, the one named last changes fastest.
Arguments:
- broadcast_ops: float32 [4, 4, 1024, 1024], P('sector', None, 'owner'), may hold values from -0.1875 to 0.1875
- resident_ops: float32 [4, 32, 1024, 1024], P('sector', 'owner'), may hold values from -6 to 6
- integrals: float32 [4, 32, 4, 4], P('sector', 'owner'), may hold values from -3 to 3
- owner_list: int32 [32, 4], P('owner'), may hold values from 0 to 3, as said below
Outputs:
- complementary: float32 [4, 32, 2, 1024, 1024], P('sector', 'owner')
The draws below stay inside these ranges and needn't reach their ends.
Inputs may be any that keep to these rules, and one draw needn't show every extreme that they name: `owner_list`: in each row one sector group is named exactly 2 times, one is not named, and every other is named once.
All inputs are finite; a program needn't handle non-finite values.
Results may differ from the reference program's by a relative error of at most 0.012.
Values may be sent and summed in bfloat16 or wider, within the bound.
A program may use at most 64 MiB of HBM per device.

```python
import jax
import jax.numpy as jnp
from jax import lax

M = 1024
NB = 4
CAP = 2
PAIRS = 4
N_SECTOR = 4
N_OWNER = 32


def draw_owner_list(key, part):
    row_keys = jax.random.split(key, N_OWNER)

    def draw_row(row_key):
        first_key, second_key = jax.random.split(row_key)
        sector_order = jax.random.permutation(first_key, N_SECTOR).astype(jnp.int32)
        row_sectors = sector_order.at[N_SECTOR - 1].set(sector_order[0])
        return jax.random.permutation(second_key, row_sectors).astype(jnp.int32)
    return jax.vmap(draw_row)(row_keys)


def block_levels(rng, dims, cuts, least, high):
    level, own = 1.0, jax.random.fold_in(rng, 6)
    for position, blocks in cuts:
        steps = jnp.exp(jax.random.uniform(jax.random.fold_in(own, position), (blocks,), jnp.float32, least / len(cuts), high / len(cuts)))
        level = level * jnp.repeat(steps, dims[position] // blocks).reshape([-1 if axis == position else 1 for axis in range(len(dims))])
    return level


def centred(stream_key, extent, width, bound, shards=(), held_as=jnp.bfloat16):
    gain = block_levels(stream_key, extent, shards, -0.22, 0.18) if shards else 1.0
    entries = jax.random.normal(stream_key, extent, jnp.float32) * width * gain
    return jnp.minimum(jnp.maximum(entries, -bound), bound).astype(held_as)


def setup_inputs(seed: int = 0) -> dict:
    arg_keys = jax.random.split(jax.random.key(seed), 5)
    return {
        "broadcast_ops": centred(arg_keys[0], (N_SECTOR, NB, M, M), M ** -0.5, 0.1875, ((0, 4), (2, 32)), jnp.float32),
        "resident_ops": centred(arg_keys[1], (N_SECTOR, N_OWNER, M, M), 1.0, 6.0, ((0, 4), (1, 32)), jnp.float32),
        "integrals": centred(arg_keys[2], (N_SECTOR, N_OWNER, PAIRS, NB), 0.5, 3.0, ((0, 4), (1, 32)), jnp.float32),
        "owner_list": draw_owner_list(jax.random.fold_in(arg_keys[4], 71), 0),
    }


def reference(broadcast_ops, resident_ops, integrals, owner_list):
    highest = lax.Precision.HIGHEST

    def owner_part(pair):
        resident, weights = pair
        return resident, weights

    pair_total = jnp.zeros((N_OWNER, PAIRS, M, M), jnp.float32)
    for sector_id in range(N_SECTOR):
        shared = broadcast_ops[sector_id]

        def one_owner(pair):
            resident, weights = pair
            products = jnp.einsum("kmj,jn->kmn", shared, resident, precision=highest)
            return jnp.einsum("pk,kmn->pmn", weights, products, precision=highest)

        partial_ops = lax.map(one_owner, (resident_ops[sector_id], integrals[sector_id]))
        rounded = lax.optimization_barrier(partial_ops.astype(jnp.bfloat16))
        pair_total = pair_total + rounded.astype(jnp.float32)
    same_owner = owner_list[:, :, None] == owner_list[:, None, :]
    earlier = jnp.arange(PAIRS)[None, :, None] < jnp.arange(PAIRS)[None, None, :]
    slot_rank = jnp.sum((same_owner & earlier).astype(jnp.int32), axis=1)
    sectors = jnp.arange(N_SECTOR)[:, None, None, None]
    slots = jnp.arange(CAP)[None, None, :, None]
    selector = ((owner_list[None, :, None, :] == sectors) & (slot_rank[None, :, None, :] == slots)).astype(jnp.float32)
    return jnp.einsum("docp,opmn->docmn", selector, pair_total, precision=highest)
```

```python
import jax
import jax.numpy as jnp
from jax import lax
from jax.experimental import pallas as pl
from jax.experimental.pallas import tpu as pltpu
from jax.sharding import PartitionSpec as P

MESH = pl.DeviceIdType.MESH
BF = jnp.bfloat16
F32 = jnp.float32
LAG = 4


def coords():
    s = lax.axis_index("sector")
    o = lax.axis_index("owner")
    return o // 8, lax.rem(o // 4, 2), lax.rem(o, 4), s // 2, lax.rem(s, 2)


def device(x, yl, z, yh, c):
    return (yh * 2 + c, lax.rem(x, 4) * 8 + yl * 4 + lax.rem(z, 4))


def kernel(b_hbm, r_hbm, wt_hbm, out_hbm, bf32, rf32, bst, ops, res, wts, wide, give, take, own, done,
           load_sem, pair_send, pair_recv, res_send, res_recv, ag_send, ag_recv, ex_send, ex_recv,
           out_sem, fin_send, fin_recv):
    x, yl, z, yh, c = coords()
    partner = device(x, yl, z, yh, 1 - c)
    y_near = device(x, 1 - yl, z, yh, c)
    y_far = device(x, yl, z, 1 - yh, c)

    def first(r):
        return device(x + (4 - r) * (1 - c), yl, z + (4 - r) * c, yh, c)

    def second(r):
        return device(x + (4 - r) * c, yl, z + (4 - r) * (1 - c), yh, c)

    def row_of(u, v, core):
        early = (u + 12) // 16
        r1 = u * (1 - early) + ((u + 8) // 3 - 4) * early
        r2 = lax.rem(u + 8, 3) * early + early
        xs = lax.rem(x + r1 * (1 - core) + r2 * core, 4)
        zs = lax.rem(z + r1 * core + r2 * (1 - core), 4)
        ys = yl * (1 - v) + (1 - yl) * v
        return pl.multiple_of((xs * 8 + ys * 4 + zs) * 32 + core * 16, 16)

    def remote(src, dst, ssem, rsem, dev):
        return pltpu.make_async_remote_copy(
            src_ref=src, dst_ref=dst, send_sem=ssem, recv_sem=rsem, device_id=dev, device_id_type=MESH
        )

    load_b = pltpu.make_async_copy(b_hbm, bf32, load_sem.at[0])
    load_b.start()
    load_w = pltpu.make_async_copy(wt_hbm, wts.at[c], load_sem.at[1])
    load_w.start()

    def load_r(i):
        part = pl.ds(i * 256, 256)
        return pltpu.make_async_copy(r_hbm.at[part], rf32.at[part], load_sem.at[2 + i])

    for i in range(4):
        load_r(i).start()

    barrier = pltpu.get_barrier_semaphore()
    peers = [partner, y_near, y_far] + [first(r) for r in (1, 2, 3)] + [second(r) for r in (1, 2, 3)]
    for peer in peers:
        pl.semaphore_signal(barrier, inc=1, device_id=peer, device_id_type=MESH)
    pl.semaphore_wait(barrier, len(peers))

    load_b.wait()
    mine = pl.ds(pl.multiple_of(c * 16, 16), 16)
    theirs = pl.ds(pl.multiple_of((1 - c) * 16, 16), 16)
    for k in range(4):
        bst[k] = bf32[k, theirs, :].astype(BF)
    send_b = remote(bst, ops.at[0, 0, c], pair_send.at[0], ag_recv.at[0], partner)
    send_b.start()
    for k in range(4):
        ops[0, 0, c, k] = bf32[k, mine, :].astype(BF)
    load_w.wait()
    send_w = remote(wts.at[c], wts.at[c], pair_send.at[1], pair_recv.at[0], partner)
    send_w.start()

    def ag_to_first(r, v):
        return remote(ops.at[0, v], ops.at[r, v], ag_send.at[24 + v * 3 + r - 1], ag_recv.at[r * 2 + v], first(r))

    def ag_to_second(u, v, r):
        to = 4 + 3 * u + r - 1
        return remote(ops.at[u, v], ops.at[to, v], ag_send.at[(u * 2 + v) * 3 + r - 1],
                      ag_recv.at[to * 2 + v], second(r))

    def arrived(u, v):
        remote(ops.at[u, v], ops.at[u, v], ag_send.at[0], ag_recv.at[u * 2 + v], partner).wait_recv()

    remote(bst, ops.at[0, 0, 1 - c], pair_send.at[0], ag_recv.at[0], partner).wait_recv()
    ag_y = remote(ops.at[0, 0], ops.at[0, 1], ag_send.at[30], ag_recv.at[1], y_near)
    ag_y.start()
    for r in (1, 3, 2):
        ag_to_first(r, 0).start()
    for r in (1, 3, 2):
        ag_to_second(0, 0, r).start()

    def send_r(i, core):
        part = pl.ds(pl.multiple_of(core * 1024 + i * 256, 256), 256)
        return remote(res.at[part], res.at[part], res_send.at[i], res_recv.at[i], partner)

    for i in range(4):
        load_r(i).wait()
        res[pl.ds(pl.multiple_of(c * 1024 + i * 256, 256), 256), :] = rf32[i * 256:(i + 1) * 256, :].astype(BF)
        send_r(i, c).start()

    arrived(0, 1)
    for r in (1, 3, 2):
        ag_to_first(r, 1).start()
    for r in (1, 3, 2):
        ag_to_second(0, 1, r).start()

    remote(wts.at[1 - c], wts.at[1 - c], pair_send.at[1], pair_recv.at[0], partner).wait_recv()
    for i in range(4):
        send_r(i, 1 - c).wait_recv()

    def exchange(u):
        return remote(give.at[u], take.at[u], ex_send.at[u], ex_recv.at[u], y_far)

    def put_own(u, v):
        return pltpu.make_async_copy(
            done.at[u, c, :, v], out_hbm.at[:, pl.ds(row_of(u, v, c), 16), :], out_sem.at[u * 2 + v])

    def put_partner(u, v, core):
        return remote(done.at[u, 1 - c, :, v], out_hbm.at[:, pl.ds(row_of(u, v, core), 16), :],
                      fin_send.at[u * 2 + v], fin_recv.at[u * 2 + v], partner)

    @pl.loop(0, 16 + LAG)
    def _(u):
        @pl.when(u < 16)
        def _():
            @pl.when(u > 0)
            def _():
                for v in range(2):
                    arrived(u, v)

            @pl.when((u > 0) & (u < 4))
            def _():
                for v in range(2):
                    for r in (1, 3, 2):
                        ag_to_second(u, v, r).start()

            for s in range(2):
                for v in range(2):
                    for half in range(2):
                        lanes = [slice(half * 512 + i * 128, half * 512 + (i + 1) * 128) for i in range(4)]
                        b = [[ops[u, v, s, k, :, lane].astype(F32) for lane in lanes] for k in range(4)]
                        for t in range(6):
                            w = [jnp.broadcast_to(wts[s, t * 4 + k:t * 4 + k + 1, :], (16, 128)) for k in range(4)]
                            for i in range(4):
                                acc = (b[0][i] * w[0] + b[1][i] * w[1]) + (b[2][i] * w[2] + b[3][i] * w[3])
                                col = s * 1024 + half * 512 + i * 128
                                wide[t * 32 + v * 16:t * 32 + v * 16 + 16, col:col + 128] = acc.astype(BF)
            for n in range(4):
                cols = slice(n * 256, (n + 1) * 256)
                part = jnp.dot(wide[...], res[:, cols], preferred_element_type=F32)
                give[u, :, cols] = part[:96].astype(BF)
                own[u, :, cols] = part[96:]
            exchange(u).start()

        @pl.when(u >= LAG)
        def _():
            w = u - LAG
            exchange(w).wait_recv()
            for t in range(2):
                for v in range(2):
                    rows = slice(t * 32 + v * 16, t * 32 + v * 16 + 16)
                    done[w, t, 0, v] = (own[w, rows, :] + take[w, rows, :].astype(F32)).astype(BF)
            for v in range(2):
                rows = slice(64 + v * 16, 64 + v * 16 + 16)
                total = own[w, rows, :] + take[w, rows, :].astype(F32)
                for t in range(2):
                    mask = jnp.broadcast_to(wts[c, 24 + t:25 + t, 0:1], (16, 1))
                    done[w, t, 1, v] = (total * mask).astype(BF)
            for v in range(2):
                put_partner(w, v, c).start()
                put_own(w, v).start()

    send_b.wait_send()
    send_w.wait_send()
    ag_y.wait_send()
    for i in range(4):
        send_r(i, c).wait_send()
    for v in range(2):
        for r in (1, 2, 3):
            ag_to_first(r, v).wait_send()

    @pl.loop(0, 4)
    def _(u):
        for v in range(2):
            for r in (1, 2, 3):
                ag_to_second(u, v, r).wait_send()

    @pl.loop(0, 16)
    def _(u):
        exchange(u).wait_send()
        for v in range(2):
            put_partner(u, v, c).wait_send()
            put_partner(u, v, 1 - c).wait_recv()
            put_own(u, v).wait()


def shards(broadcast_ops, resident_ops, integrals, owner_list):
    weights = integrals[0, 0]
    owners = owner_list[0]
    pairs = jnp.arange(4)
    rank = jnp.sum(((owners[:, None] == owners[None, :]) & (pairs[:, None] < pairs[None, :])).astype(jnp.int32), axis=0)
    half = lax.axis_index("sector") // 2
    slots = []
    for h in (1 - half, half):
        slots.append((owners == 2 * h) & (rank == 0))
        slots.append((owners == 2 * h + 1) & (rank == 0))
        slots.append((owners // 2 == h) & (rank == 1))
    select = jnp.stack(slots)
    slot_weights = jnp.sum(jnp.where(select[:, :, None], weights[None], 0.0), axis=1)
    masks = jnp.stack([jnp.any((owners == 2 * half + t) & (rank == 1)) for t in range(2)]).astype(F32)
    table = jnp.concatenate([slot_weights.reshape(24), masks, jnp.zeros((6,), F32)])
    table = jnp.broadcast_to(table[:, None], (32, 128))
    hbm = pl.BlockSpec(memory_space=pl.ANY)
    dma = pltpu.SemaphoreType.DMA
    result = pl.pallas_call(
        kernel,
        out_shape=jax.ShapeDtypeStruct((2, 1024, 1024), BF),
        in_specs=[hbm, hbm, hbm],
        out_specs=hbm,
        scratch_shapes=[
            pltpu.VMEM((4, 32, 1024), F32),
            pltpu.VMEM((1024, 1024), F32),
            pltpu.VMEM((4, 16, 1024), BF),
            pltpu.VMEM((16, 2, 2, 4, 16, 1024), BF),
            pltpu.VMEM((2048, 1024), BF),
            pltpu.VMEM((2, 32, 128), F32),
            pltpu.VMEM((192, 2048), BF),
            pltpu.VMEM((16, 96, 1024), BF),
            pltpu.VMEM((16, 96, 1024), BF),
            pltpu.VMEM((16, 96, 1024), F32),
            pltpu.VMEM((16, 2, 2, 2, 16, 1024), BF),
            dma((6,)), dma((2,)), dma((1,)), dma((4,)), dma((4,)), dma((31,)), dma((32,)), dma((16,)), dma((16,)),
            dma((32,)), dma((32,)), dma((32,)),
        ],
        compiler_params=pltpu.CompilerParams(
            collective_id=0, has_side_effects=True, vmem_limit_bytes=56 * 2**20
        ),
    )(broadcast_ops[0], resident_ops[0, 0], table)
    return result.astype(F32)[None, None]


def solution(mesh):
    in_specs = (
        P("sector", None, "owner", None),
        P("sector", "owner", None, None),
        P("sector", "owner", None, None),
        P("owner", None),
    )
    out_specs = P("sector", "owner", None, None, None)
    return jax.shard_map(shards, mesh=mesh, in_specs=in_specs, out_specs=out_specs, check_vma=False)
```

```python
import jax
import jax.numpy as jnp
from jax import lax
from jax.experimental import pallas as pl
from jax.experimental.pallas import tpu as pltpu
from jax.sharding import PartitionSpec as P

MESH = pl.DeviceIdType.MESH
BF = jnp.bfloat16
F32 = jnp.float32
STEPS = 32
LAG = 9


def coords():
    s = lax.axis_index("sector")
    o = lax.axis_index("owner")
    return o // 8, lax.rem(o // 4, 2), lax.rem(o, 4), s // 2, lax.rem(s, 2)


def device(x, yl, z, yh, c):
    return (yh * 2 + c, lax.rem(x, 4) * 8 + yl * 4 + lax.rem(z, 4))


ORDER = (
    [(0, 0, 0), (1, 0, 0), (3, 0, 0), (0, 1, 0), (0, 3, 0), (0, 0, 1)]
    + [(1, 1, 0), (1, 3, 0), (3, 1, 0), (3, 3, 0), (1, 0, 1), (3, 0, 1), (0, 1, 1), (0, 3, 1), (2, 0, 0), (0, 2, 0)]
    + [(1, 1, 1), (1, 3, 1), (3, 1, 1), (3, 3, 1), (1, 2, 0), (3, 2, 0), (2, 1, 0), (2, 3, 0), (2, 0, 1), (0, 2, 1)]
    + [(1, 2, 1), (3, 2, 1), (2, 1, 1), (2, 3, 1), (2, 2, 0), (2, 2, 1)]
)
STEP = {at: i for i, at in enumerate(ORDER)}
SENDS = {
    1: [(2, 1, 0, 1), (2, 1, 0, 3)],
    2: [(2, 3, 0, 1), (2, 3, 0, 3)],
    5: [(1, 0, 1, 1), (1, 0, 1, 3), (2, 0, 1, 1), (2, 0, 1, 3)],
    6: [(1, 0, 0, 2), (2, 0, 0, 2)],
    10: [(2, 1, 1, 1), (2, 1, 1, 3)],
    11: [(2, 3, 1, 1), (2, 3, 1, 3)],
    12: [(2, 1, 0, 2), (2, 3, 0, 2)],
    14: [(2, 2, 0, 1), (2, 2, 0, 3)],
    15: [(1, 0, 1, 2), (2, 0, 1, 2)],
    17: [(2, 1, 1, 2), (2, 3, 1, 2)],
    18: [(2, 2, 0, 2)],
    24: [(2, 2, 1, 1), (2, 2, 1, 3)],
    25: [(2, 2, 1, 2)],
}
FIRST_SENDS = [(1, 0, 0, 1), (1, 0, 0, 3), (2, 0, 0, 1), (2, 0, 0, 3)]
ALL_SENDS = FIRST_SENDS + [send for sends in SENDS.values() for send in sends]


def parts(i):
    if isinstance(i, int):
        return ORDER[i]
    codes = [r1 + 4 * r2 + 16 * v for r1, r2, v in ORDER]
    code = codes[0]
    for n in range(1, STEPS):
        code = code + lax.div(i + (STEPS - n), STEPS) * (codes[n] - codes[n - 1])
    return lax.rem(code, 4), lax.rem(lax.div(code, 4), 4), lax.div(code, 16)


def kernel(b_hbm, r_hbm, w_hbm, o_hbm, out, bf32, rf32, bst, ops, res, table, owners, wts, wide, give, take, own, done,
           load_sem, pair_send, pair_recv, res_send, res_recv, ag_send, ag_recv, ex_send, ex_recv, fin_send, fin_recv):
    x, yl, z, yh, c = coords()
    partner = device(x, yl, z, yh, 1 - c)
    y_near = device(x, 1 - yl, z, yh, c)
    y_far = device(x, yl, z, 1 - yh, c)

    def first(r):
        return device(x + (4 - r) * (1 - c), yl, z + (4 - r) * c, yh, c)

    def second(r):
        return device(x + (4 - r) * c, yl, z + (4 - r) * (1 - c), yh, c)

    def rows_of(i, core):
        r1, r2, v = parts(i)
        xs = lax.rem(x + r1 * (1 - core) + r2 * core, 4)
        zs = lax.rem(z + r1 * core + r2 * (1 - core), 4)
        ys = yl * (1 - v) + (1 - yl) * v
        return pl.ds(pl.multiple_of((xs * 8 + ys * 4 + zs) * 32 + core * 16, 16), 16)

    def remote(src, dst, ssem, rsem, dev):
        return pltpu.make_async_remote_copy(
            src_ref=src, dst_ref=dst, send_sem=ssem, recv_sem=rsem, device_id=dev, device_id_type=MESH
        )

    load_b = pltpu.make_async_copy(b_hbm, bf32, load_sem.at[0])
    load_b.start()
    load_w = pltpu.make_async_copy(w_hbm, table, load_sem.at[1])
    load_w.start()
    load_o = pltpu.make_async_copy(o_hbm, owners, load_sem.at[2])
    load_o.start()

    def load_r(i):
        part = pl.ds(i * 256, 256)
        return pltpu.make_async_copy(r_hbm.at[part], rf32.at[part], load_sem.at[3 + i])

    for i in range(4):
        load_r(i).start()

    barrier = pltpu.get_barrier_semaphore()
    peers = [partner, y_near, y_far] + [first(r) for r in (1, 2, 3)] + [second(r) for r in (1, 2, 3)]
    for peer in peers:
        pl.semaphore_signal(barrier, inc=1, device_id=peer, device_id_type=MESH)

    load_b.wait()
    mine = pl.ds(pl.multiple_of(c * 16, 16), 16)
    theirs = pl.ds(pl.multiple_of((1 - c) * 16, 16), 16)
    for k in range(4):
        bst[k] = bf32[k, theirs, :].astype(BF)
    for k in range(4):
        ops[0, c, k] = bf32[k, mine, :].astype(BF)

    load_w.wait()
    load_o.wait()
    owner = [owners[p] for p in range(4)]
    one, zero = jnp.float32(1), jnp.float32(0)
    twice = [sum([(jnp.where(owner[q] == owner[p], one, zero)) for q in range(p)], zero) for p in range(4)]
    row = 0
    for half in (1 - yh, yh):
        for t in range(3):
            if t < 2:
                pick = [jnp.where(owner[p] == 2 * half + t, one, zero) * (one - twice[p]) for p in range(4)]
            else:
                pick = [jnp.where(owner[p] // 2 == half, one, zero) * twice[p] for p in range(4)]
            for k in range(4):
                value = (pick[0] * table[0, k] + pick[1] * table[1, k]) + (pick[2] * table[2, k] + pick[3] * table[3, k])
                wts[c, row:row + 1, :] = jnp.full((1, 128), value, F32)
                row += 1
    for t in range(2):
        flag = sum([jnp.where(owner[p] == 2 * yh + t, one, zero) * twice[p] for p in range(4)], zero)
        wts[c, 24 + t:25 + t, :] = jnp.full((1, 128), flag, F32)

    pl.semaphore_wait(barrier, len(peers))
    send_b = remote(bst, ops.at[0, c], pair_send.at[0], ag_recv.at[0], partner)
    send_b.start()
    send_w = remote(wts.at[c], wts.at[c], pair_send.at[1], pair_recv.at[0], partner)
    send_w.start()

    def gather(send):
        axis, r1, v, r = send
        to, dev = (STEP[r, 0, v], first(r)) if axis == 1 else (STEP[r1, r, v], second(r))
        return remote(ops.at[STEP[r1, 0, v]], ops.at[to], ag_send.at[ALL_SENDS.index(send)], ag_recv.at[to], dev)

    def arrived(i):
        remote(ops.at[i], ops.at[i], ag_send.at[0], ag_recv.at[i], partner).wait_recv()

    def send_r(i, core):
        part = pl.ds(pl.multiple_of(core * 1024 + i * 256, 256), 256)
        return remote(res.at[part], res.at[part], res_send.at[i], res_recv.at[i], partner)

    def put_r(i):
        load_r(i).wait()
        res[pl.ds(pl.multiple_of(c * 1024 + i * 256, 256), 256), :] = rf32[i * 256:(i + 1) * 256, :].astype(BF)
        send_r(i, c).start()

    def ag_y(core, n):
        return remote(ops.at[0, core], ops.at[5, core], ag_send.at[30 + n], ag_recv.at[5 + 27 * n], y_near)

    ag_y(c, 0).start()
    put_r(0)
    remote(bst, ops.at[0, 1 - c], pair_send.at[0], ag_recv.at[0], partner).wait_recv()
    ag_y(1 - c, 1).start()
    for send in FIRST_SENDS:
        gather(send).start()
    for i in range(1, 4):
        put_r(i)

    remote(wts.at[1 - c], wts.at[1 - c], pair_send.at[1], pair_recv.at[0], partner).wait_recv()
    for i in range(4):
        send_r(i, 1 - c).wait_recv()

    def exchange(i):
        return remote(give.at[i], take.at[i], ex_send.at[i], ex_recv.at[i], y_far)

    def put_partner(i, rows):
        return remote(done.at[i], out.at[:, rows, :], fin_send.at[i], fin_recv.at[i], partner)

    @pl.loop(0, STEPS + LAG)
    def _(i):
        @pl.when(i < STEPS)
        def _():
            @pl.when(((i > 0) & (i < 5)) | (i > 5))
            def _():
                arrived(i)

            @pl.when(i == 5)
            def _():
                ag_y(c, 0).wait_recv()
                ag_y(1 - c, 1).wait_recv()

            for step, sends in SENDS.items():
                @pl.when(i == step)
                def _():
                    for send in sends:
                        gather(send).start()

            for s in range(2):
                for half in range(2):
                    lanes = [slice(half * 512 + n * 128, half * 512 + (n + 1) * 128) for n in range(4)]
                    b = [[ops[i, s, k, :, lane].astype(F32) for lane in lanes] for k in range(4)]
                    for t in range(6):
                        w = [jnp.broadcast_to(wts[s, t * 4 + k:t * 4 + k + 1, :], (16, 128)) for k in range(4)]
                        for n in range(4):
                            acc = (b[0][n] * w[0] + b[1][n] * w[1]) + (b[2][n] * w[2] + b[3][n] * w[3])
                            col = s * 1024 + half * 512 + n * 128
                            wide[t * 16:t * 16 + 16, col:col + 128] = acc.astype(BF)
            for n in range(4):
                cols = slice(n * 256, (n + 1) * 256)
                part = jnp.dot(wide[...], res[:, cols], preferred_element_type=F32)
                give[i, :, cols] = part[:48].astype(BF)
                own[i, :, cols] = part[48:]
            exchange(i).start()

        @pl.when(i >= LAG)
        def _():
            w = i - LAG
            exchange(w).wait_recv()
            firsts = [own[w, t * 16:t * 16 + 16, :] + take[w, t * 16:t * 16 + 16, :].astype(F32) for t in range(2)]
            extra = own[w, 32:48, :] + take[w, 32:48, :].astype(F32)
            mask = [jnp.broadcast_to(wts[c, 24 + t:25 + t, 0:1], (16, 1)) for t in range(2)]
            even = lax.rem(c + 1, 2).astype(F32)
            odd = c.astype(F32)
            done[w, 0] = (firsts[0] * odd + firsts[1] * even)
            done[w, 1] = (extra * (mask[0] * odd + mask[1] * even))
            rows = rows_of(w, c)
            put_partner(w, rows).start()
            out[0, rows, :] = (firsts[0] * even + firsts[1] * odd)
            out[1, rows, :] = (extra * (mask[0] * even + mask[1] * odd))

    send_b.wait_send()
    send_w.wait_send()
    ag_y(c, 0).wait_send()
    ag_y(1 - c, 1).wait_send()
    for i in range(4):
        send_r(i, c).wait_send()
    for send in ALL_SENDS:
        gather(send).wait_send()

    @pl.loop(0, STEPS)
    def _(i):
        exchange(i).wait_send()

    for i in range(STEPS):
        put_partner(i, rows_of(i, c)).wait_send()
        put_partner(i, rows_of(i, 1 - c)).wait_recv()


def shards(broadcast_ops, resident_ops, integrals, owner_list):
    hbm = pl.BlockSpec(memory_space=pltpu.HBM)
    dma = pltpu.SemaphoreType.DMA
    result = pl.pallas_call(
        kernel,
        out_shape=OUT,
        in_specs=[hbm, hbm, hbm, hbm],
        out_specs=pl.BlockSpec(memory_space=pltpu.VMEM),
        scratch_shapes=[
            pltpu.VMEM((4, 32, 1024), F32),
            pltpu.VMEM((1024, 1024), F32),
            pltpu.VMEM((4, 16, 1024), BF),
            pltpu.VMEM((STEPS, 2, 4, 16, 1024), BF),
            pltpu.VMEM((2048, 1024), BF),
            pltpu.SMEM((4, 4), F32),
            pltpu.SMEM((4,), jnp.int32),
            pltpu.VMEM((2, 32, 128), F32),
            pltpu.VMEM((96, 2048), BF),
            pltpu.VMEM((STEPS, 48, 1024), BF),
            pltpu.VMEM((STEPS, 48, 1024), BF),
            pltpu.VMEM((STEPS, 48, 1024), F32),
            pltpu.VMEM((STEPS, 2, 16, 1024), F32),
            dma((7,)), dma((2,)), dma((1,)), dma((4,)), dma((4,)), dma((32,)), dma((STEPS + 1,)), dma((STEPS,)),
            dma((STEPS,)), dma((STEPS,)), dma((STEPS,)),
        ],
        compiler_params=pltpu.CompilerParams(
            collective_id=0, has_side_effects=True, vmem_limit_bytes=67043328 - 8388608
        ),
    )(broadcast_ops[0], resident_ops[0, 0], integrals[0, 0], owner_list[0])
    return result[None, None]


OUT = pltpu.VMEM((2, 1024, 1024), F32)


def solution(mesh):
    in_specs = (
        P("sector", None, "owner", None),
        P("sector", "owner", None, None),
        P("sector", "owner", None, None),
        P("owner", None),
    )
    out_specs = P("sector", "owner", None, None, None)
    return jax.shard_map(shards, mesh=mesh, in_specs=in_specs, out_specs=out_specs, check_vma=False)
```

```python
import jax
import jax.numpy as jnp
from jax import lax
from jax.experimental import pallas as pl
from jax.experimental.pallas import tpu as pltpu
from jax.sharding import PartitionSpec as P

MESH = pl.DeviceIdType.MESH
BF = jnp.bfloat16
F32 = jnp.float32
STEPS = 32
LAG = 9


def coords():
    s = lax.axis_index("sector")
    o = lax.axis_index("owner")
    return o // 8, lax.rem(o // 4, 2), lax.rem(o, 4), s // 2, lax.rem(s, 2)


def device(x, yl, z, yh, c):
    return (yh * 2 + c, lax.rem(x, 4) * 8 + yl * 4 + lax.rem(z, 4))


ORDER = (
    [(0, 0, 0), (1, 0, 0), (3, 0, 0), (0, 1, 0), (0, 3, 0), (0, 0, 1)]
    + [(1, 1, 0), (1, 3, 0), (3, 1, 0), (3, 3, 0), (1, 0, 1), (3, 0, 1), (0, 1, 1), (0, 3, 1), (2, 0, 0), (0, 2, 0)]
    + [(1, 1, 1), (1, 3, 1), (3, 1, 1), (3, 3, 1), (1, 2, 0), (3, 2, 0), (2, 1, 0), (2, 3, 0), (2, 0, 1), (0, 2, 1)]
    + [(1, 2, 1), (3, 2, 1), (2, 1, 1), (2, 3, 1), (2, 2, 0), (2, 2, 1)]
)
STEP = {at: i for i, at in enumerate(ORDER)}
SENDS = {
    0: [(2, 0, 0, 1), (2, 0, 0, 3)],
    1: [(2, 1, 0, 1), (2, 1, 0, 3)],
    2: [(2, 3, 0, 1), (2, 3, 0, 3)],
    5: [(1, 0, 1, 1), (1, 0, 1, 3), (2, 0, 1, 1), (2, 0, 1, 3)],
    6: [(1, 0, 0, 2), (2, 0, 0, 2)],
    10: [(2, 1, 1, 1), (2, 1, 1, 3)],
    11: [(2, 3, 1, 1), (2, 3, 1, 3)],
    12: [(2, 1, 0, 2), (2, 3, 0, 2)],
    14: [(2, 2, 0, 1), (2, 2, 0, 3)],
    15: [(1, 0, 1, 2), (2, 0, 1, 2)],
    17: [(2, 1, 1, 2), (2, 3, 1, 2)],
    18: [(2, 2, 0, 2)],
    24: [(2, 2, 1, 1), (2, 2, 1, 3)],
    25: [(2, 2, 1, 2)],
}
FIRST_SENDS = [(1, 0, 0, 1), (1, 0, 0, 3)]
ALL_SENDS = FIRST_SENDS + [send for sends in SENDS.values() for send in sends]


def parts(i):
    if isinstance(i, int):
        return ORDER[i]
    codes = [r1 + 4 * r2 + 16 * v for r1, r2, v in ORDER]
    code = codes[0]
    for n in range(1, STEPS):
        code = code + lax.div(i + (STEPS - n), STEPS) * (codes[n] - codes[n - 1])
    return lax.rem(code, 4), lax.rem(lax.div(code, 4), 4), lax.div(code, 16)


def kernel(b_hbm, r_hbm, w_hbm, o_hbm, out, bf32, rf32, bst, ops, res, table, owners, wts, wide, give, take, own, done,
           load_sem, pair_send, pair_recv, res_send, res_recv, ag_send, ag_recv, ex_send, ex_recv, fin_send, fin_recv):
    x, yl, z, yh, c = coords()
    partner = device(x, yl, z, yh, 1 - c)
    y_near = device(x, 1 - yl, z, yh, c)
    y_far = device(x, yl, z, 1 - yh, c)

    def first(r):
        return device(x + (4 - r) * (1 - c), yl, z + (4 - r) * c, yh, c)

    def second(r):
        return device(x + (4 - r) * c, yl, z + (4 - r) * (1 - c), yh, c)

    def rows_of(i, core):
        r1, r2, v = parts(i)
        xs = lax.rem(x + r1 * (1 - core) + r2 * core, 4)
        zs = lax.rem(z + r1 * core + r2 * (1 - core), 4)
        ys = yl * (1 - v) + (1 - yl) * v
        return pl.ds(pl.multiple_of((xs * 8 + ys * 4 + zs) * 32 + core * 16, 16), 16)

    def remote(src, dst, ssem, rsem, dev):
        return pltpu.make_async_remote_copy(
            src_ref=src, dst_ref=dst, send_sem=ssem, recv_sem=rsem, device_id=dev, device_id_type=MESH
        )

    load_b = pltpu.make_async_copy(b_hbm, bf32, load_sem.at[0])
    load_b.start()
    load_w = pltpu.make_async_copy(w_hbm, table, load_sem.at[1])
    load_w.start()
    load_o = pltpu.make_async_copy(o_hbm, owners, load_sem.at[2])
    load_o.start()

    def load_r(i):
        part = pl.ds(i * 256, 256)
        return pltpu.make_async_copy(r_hbm.at[part], rf32.at[part], load_sem.at[3 + i])

    for i in range(4):
        load_r(i).start()

    barrier = pltpu.get_barrier_semaphore()
    peers = [partner, y_near, y_far] + [first(r) for r in (1, 2, 3)] + [second(r) for r in (1, 2, 3)]
    for peer in peers:
        pl.semaphore_signal(barrier, inc=1, device_id=peer, device_id_type=MESH)

    load_b.wait()
    mine = pl.ds(pl.multiple_of(c * 16, 16), 16)
    theirs = pl.ds(pl.multiple_of((1 - c) * 16, 16), 16)
    for k in range(4):
        bst[k] = bf32[k, theirs, :].astype(BF)
    for k in range(4):
        ops[0, c, k] = bf32[k, mine, :].astype(BF)

    load_w.wait()
    load_o.wait()
    owner = [owners[p] for p in range(4)]
    one, zero = jnp.float32(1), jnp.float32(0)
    twice = [sum([(jnp.where(owner[q] == owner[p], one, zero)) for q in range(p)], zero) for p in range(4)]
    row = 0
    for half in (1 - yh, yh):
        for t in range(3):
            if t < 2:
                pick = [jnp.where(owner[p] == 2 * half + t, one, zero) * (one - twice[p]) for p in range(4)]
            else:
                pick = [jnp.where(owner[p] // 2 == half, one, zero) * twice[p] for p in range(4)]
            for k in range(4):
                value = (pick[0] * table[0, k] + pick[1] * table[1, k]) + (pick[2] * table[2, k] + pick[3] * table[3, k])
                wts[c, row:row + 1, :] = jnp.full((1, 128), value, F32)
                row += 1
    for t in range(2):
        flag = sum([jnp.where(owner[p] == 2 * yh + t, one, zero) * twice[p] for p in range(4)], zero)
        wts[c, 24 + t:25 + t, :] = jnp.full((1, 128), flag, F32)

    for i in range(4):
        load_r(i).wait()
        res[pl.ds(pl.multiple_of(c * 1024 + i * 256, 256), 256), :] = rf32[i * 256:(i + 1) * 256, :].astype(BF)

    pl.semaphore_wait(barrier, len(peers))
    send_b = remote(bst, ops.at[0, c], pair_send.at[0], ag_recv.at[0], partner)
    send_b.start()
    send_w = remote(wts.at[c], wts.at[c], pair_send.at[1], pair_recv.at[0], partner)
    send_w.start()

    def gather(send):
        axis, r1, v, r = send
        to, dev = (STEP[r, 0, v], first(r)) if axis == 1 else (STEP[r1, r, v], second(r))
        return remote(ops.at[STEP[r1, 0, v]], ops.at[to], ag_send.at[ALL_SENDS.index(send)], ag_recv.at[to], dev)

    def arrived(i):
        remote(ops.at[i], ops.at[i], ag_send.at[0], ag_recv.at[i], partner).wait_recv()

    def send_r(i, core):
        part = pl.ds(pl.multiple_of(core * 1024 + i * 256, 256), 256)
        return remote(res.at[part], res.at[part], res_send.at[i], res_recv.at[i], partner)

    def ag_y(core, n):
        return remote(ops.at[0, core], ops.at[5, core], ag_send.at[30 + n], ag_recv.at[5 + 27 * n], y_near)

    ag_y(c, 0).start()
    for i in range(4):
        send_r(i, c).start()
    remote(bst, ops.at[0, 1 - c], pair_send.at[0], ag_recv.at[0], partner).wait_recv()
    ag_y(1 - c, 1).start()
    for send in FIRST_SENDS:
        gather(send).start()

    remote(wts.at[1 - c], wts.at[1 - c], pair_send.at[1], pair_recv.at[0], partner).wait_recv()
    for i in range(4):
        send_r(i, 1 - c).wait_recv()

    def exchange(i):
        return remote(give.at[i], take.at[i], ex_send.at[i], ex_recv.at[i], y_far)

    def put_partner(i, rows):
        return remote(done.at[i], out.at[:, rows, :], fin_send.at[i], fin_recv.at[i], partner)

    @pl.loop(0, STEPS + LAG)
    def _(i):
        @pl.when(i < STEPS)
        def _():
            @pl.when(((i > 0) & (i < 5)) | (i > 5))
            def _():
                arrived(i)

            @pl.when(i == 5)
            def _():
                ag_y(c, 0).wait_recv()
                ag_y(1 - c, 1).wait_recv()

            for step, sends in SENDS.items():
                @pl.when(i == step)
                def _():
                    for send in sends:
                        gather(send).start()

            for s in range(2):
                for half in range(2):
                    lanes = [slice(half * 512 + n * 128, half * 512 + (n + 1) * 128) for n in range(4)]
                    b = [[ops[i, s, k, :, lane].astype(F32) for lane in lanes] for k in range(4)]
                    for t in range(6):
                        w = [jnp.broadcast_to(wts[s, t * 4 + k:t * 4 + k + 1, :], (16, 128)) for k in range(4)]
                        for n in range(4):
                            acc = (b[0][n] * w[0] + b[1][n] * w[1]) + (b[2][n] * w[2] + b[3][n] * w[3])
                            col = s * 1024 + half * 512 + n * 128
                            wide[t * 16:t * 16 + 16, col:col + 128] = acc.astype(BF)
            for n in range(4):
                cols = slice(n * 256, (n + 1) * 256)
                part = jnp.dot(wide[...], res[:, cols], preferred_element_type=F32)
                give[i, :, cols] = part[:48].astype(BF)
                own[i, :, cols] = part[48:]
            exchange(i).start()

        @pl.when(i >= LAG)
        def _():
            w = i - LAG
            exchange(w).wait_recv()
            firsts = [own[w, t * 16:t * 16 + 16, :] + take[w, t * 16:t * 16 + 16, :].astype(F32) for t in range(2)]
            extra = own[w, 32:48, :] + take[w, 32:48, :].astype(F32)
            mask = [jnp.broadcast_to(wts[c, 24 + t:25 + t, 0:1], (16, 1)) for t in range(2)]
            even = lax.rem(c + 1, 2).astype(F32)
            odd = c.astype(F32)
            done[w, 0] = (firsts[0] * odd + firsts[1] * even)
            done[w, 1] = (extra * (mask[0] * odd + mask[1] * even))
            rows = rows_of(w, c)
            put_partner(w, rows).start()
            out[0, rows, :] = (firsts[0] * even + firsts[1] * odd)
            out[1, rows, :] = (extra * (mask[0] * even + mask[1] * odd))

    send_b.wait_send()
    send_w.wait_send()
    ag_y(c, 0).wait_send()
    ag_y(1 - c, 1).wait_send()
    for i in range(4):
        send_r(i, c).wait_send()
    for send in ALL_SENDS:
        gather(send).wait_send()

    @pl.loop(0, STEPS)
    def _(i):
        exchange(i).wait_send()

    for i in range(STEPS):
        put_partner(i, rows_of(i, c)).wait_send()
        put_partner(i, rows_of(i, 1 - c)).wait_recv()


def shards(broadcast_ops, resident_ops, integrals, owner_list):
    hbm = pl.BlockSpec(memory_space=pltpu.HBM)
    dma = pltpu.SemaphoreType.DMA
    result = pl.pallas_call(
        kernel,
        out_shape=OUT,
        in_specs=[hbm, hbm, hbm, hbm],
        out_specs=pl.BlockSpec(memory_space=pltpu.VMEM),
        scratch_shapes=[
            pltpu.VMEM((4, 32, 1024), F32),
            pltpu.VMEM((1024, 1024), F32),
            pltpu.VMEM((4, 16, 1024), BF),
            pltpu.VMEM((STEPS, 2, 4, 16, 1024), BF),
            pltpu.VMEM((2048, 1024), BF),
            pltpu.SMEM((4, 4), F32),
            pltpu.SMEM((4,), jnp.int32),
            pltpu.VMEM((2, 32, 128), F32),
            pltpu.VMEM((96, 2048), BF),
            pltpu.VMEM((STEPS, 48, 1024), BF),
            pltpu.VMEM((STEPS, 48, 1024), BF),
            pltpu.VMEM((STEPS, 48, 1024), F32),
            pltpu.VMEM((STEPS, 2, 16, 1024), F32),
            dma((7,)), dma((2,)), dma((1,)), dma((4,)), dma((4,)), dma((32,)), dma((STEPS + 1,)), dma((STEPS,)),
            dma((STEPS,)), dma((STEPS,)), dma((STEPS,)),
        ],
        compiler_params=pltpu.CompilerParams(
            collective_id=0, has_side_effects=True, vmem_limit_bytes=67043328 - 8388608
        ),
    )(broadcast_ops[0], resident_ops[0, 0], integrals[0, 0], owner_list[0])
    return result[None, None]


OUT = pltpu.VMEM((2, 1024, 1024), F32)


def solution(mesh):
    in_specs = (
        P("sector", None, "owner", None),
        P("sector", "owner", None, None),
        P("sector", "owner", None, None),
        P("owner", None),
    )
    out_specs = P("sector", "owner", None, None, None)
    return jax.shard_map(shards, mesh=mesh, in_specs=in_specs, out_specs=out_specs, check_vma=False)
```

```python
import jax
import jax.numpy as jnp
from jax import lax
from jax.experimental import pallas as pl
from jax.experimental.pallas import tpu as pltpu
from jax.sharding import PartitionSpec as P

MESH = pl.DeviceIdType.MESH
BF = jnp.bfloat16
F32 = jnp.float32
STEPS = 32
LAG = 9


def coords():
    s = lax.axis_index("sector")
    o = lax.axis_index("owner")
    return o // 8, lax.rem(o // 4, 2), lax.rem(o, 4), s // 2, lax.rem(s, 2)


def device(x, yl, z, yh, c):
    return (yh * 2 + c, lax.rem(x, 4) * 8 + yl * 4 + lax.rem(z, 4))


ORDER = (
    [(0, 0, 0), (1, 0, 0), (3, 0, 0), (0, 0, 1), (0, 1, 0), (0, 3, 0)]
    + [(1, 1, 0), (1, 3, 0), (3, 1, 0), (3, 3, 0), (1, 0, 1), (3, 0, 1), (0, 1, 1), (0, 3, 1), (2, 0, 0), (0, 2, 0)]
    + [(1, 1, 1), (1, 3, 1), (3, 1, 1), (3, 3, 1), (1, 2, 0), (3, 2, 0), (2, 1, 0), (2, 3, 0), (2, 0, 1), (0, 2, 1)]
    + [(1, 2, 1), (3, 2, 1), (2, 1, 1), (2, 3, 1), (2, 2, 0), (2, 2, 1)]
)
STEP = {at: i for i, at in enumerate(ORDER)}
SENDS = {
    0: [(2, 0, 0, 1), (2, 0, 0, 3)],
    1: [(2, 1, 0, 1), (2, 1, 0, 3)],
    2: [(2, 3, 0, 1), (2, 3, 0, 3)],
    3: [(1, 0, 1, 1), (1, 0, 1, 3), (2, 0, 1, 1), (2, 0, 1, 3)],
    6: [(1, 0, 0, 2), (2, 0, 0, 2)],
    10: [(2, 1, 1, 1), (2, 1, 1, 3)],
    11: [(2, 3, 1, 1), (2, 3, 1, 3)],
    12: [(2, 1, 0, 2), (2, 3, 0, 2)],
    14: [(2, 2, 0, 1), (2, 2, 0, 3)],
    15: [(1, 0, 1, 2), (2, 0, 1, 2)],
    17: [(2, 1, 1, 2), (2, 3, 1, 2)],
    18: [(2, 2, 0, 2)],
    24: [(2, 2, 1, 1), (2, 2, 1, 3)],
    25: [(2, 2, 1, 2)],
}
FIRST_SENDS = [(1, 0, 0, 1), (1, 0, 0, 3)]
ALL_SENDS = FIRST_SENDS + [send for sends in SENDS.values() for send in sends]


def parts(i):
    if isinstance(i, int):
        return ORDER[i]
    codes = [r1 + 4 * r2 + 16 * v for r1, r2, v in ORDER]
    code = codes[0]
    for n in range(1, STEPS):
        code = code + lax.div(i + (STEPS - n), STEPS) * (codes[n] - codes[n - 1])
    return lax.rem(code, 4), lax.rem(lax.div(code, 4), 4), lax.div(code, 16)


def kernel(b_hbm, r_hbm, w_hbm, o_hbm, out, bf32, rf32, bst, ops, res, table, owners, wts, wide, give, take, own, done,
           load_sem, pair_send, pair_recv, res_send, res_recv, ag_send, ag_recv, ex_send, ex_recv, fin_send, fin_recv):
    x, yl, z, yh, c = coords()
    partner = device(x, yl, z, yh, 1 - c)
    y_near = device(x, 1 - yl, z, yh, c)
    y_far = device(x, yl, z, 1 - yh, c)

    def first(r):
        return device(x + (4 - r) * (1 - c), yl, z + (4 - r) * c, yh, c)

    def second(r):
        return device(x + (4 - r) * c, yl, z + (4 - r) * (1 - c), yh, c)

    def rows_of(i, core):
        r1, r2, v = parts(i)
        xs = lax.rem(x + r1 * (1 - core) + r2 * core, 4)
        zs = lax.rem(z + r1 * core + r2 * (1 - core), 4)
        ys = yl * (1 - v) + (1 - yl) * v
        return pl.ds(pl.multiple_of((xs * 8 + ys * 4 + zs) * 32 + core * 16, 16), 16)

    def remote(src, dst, ssem, rsem, dev):
        return pltpu.make_async_remote_copy(
            src_ref=src, dst_ref=dst, send_sem=ssem, recv_sem=rsem, device_id=dev, device_id_type=MESH
        )

    load_b = pltpu.make_async_copy(b_hbm, bf32, load_sem.at[0])
    load_b.start()
    load_w = pltpu.make_async_copy(w_hbm, table, load_sem.at[1])
    load_w.start()
    load_o = pltpu.make_async_copy(o_hbm, owners, load_sem.at[2])
    load_o.start()

    def load_r(i):
        part = pl.ds(i * 256, 256)
        return pltpu.make_async_copy(r_hbm.at[part], rf32.at[part], load_sem.at[3 + i])

    for i in range(4):
        load_r(i).start()

    barrier = pltpu.get_barrier_semaphore()
    peers = [partner, y_near, y_far] + [first(r) for r in (1, 2, 3)] + [second(r) for r in (1, 2, 3)]
    for peer in peers:
        pl.semaphore_signal(barrier, inc=1, device_id=peer, device_id_type=MESH)

    load_b.wait()
    mine = pl.ds(pl.multiple_of(c * 16, 16), 16)
    theirs = pl.ds(pl.multiple_of((1 - c) * 16, 16), 16)
    for k in range(4):
        bst[k] = bf32[k, theirs, :].astype(BF)
    for k in range(4):
        ops[0, c, k] = bf32[k, mine, :].astype(BF)

    load_w.wait()
    load_o.wait()
    owner = [owners[p] for p in range(4)]
    one, zero = jnp.float32(1), jnp.float32(0)
    twice = [sum([(jnp.where(owner[q] == owner[p], one, zero)) for q in range(p)], zero) for p in range(4)]
    row = 0
    for half in (1 - yh, yh):
        for t in range(3):
            if t < 2:
                pick = [jnp.where(owner[p] == 2 * half + t, one, zero) * (one - twice[p]) for p in range(4)]
            else:
                pick = [jnp.where(owner[p] // 2 == half, one, zero) * twice[p] for p in range(4)]
            for k in range(4):
                value = (pick[0] * table[0, k] + pick[1] * table[1, k]) + (pick[2] * table[2, k] + pick[3] * table[3, k])
                wts[c, row:row + 1, :] = jnp.full((1, 128), value, F32)
                row += 1
    for t in range(2):
        flag = sum([jnp.where(owner[p] == 2 * yh + t, one, zero) * twice[p] for p in range(4)], zero)
        wts[c, 24 + t:25 + t, :] = jnp.full((1, 128), flag, F32)

    for i in range(4):
        load_r(i).wait()
        res[pl.ds(pl.multiple_of(c * 1024 + i * 256, 256), 256), :] = rf32[i * 256:(i + 1) * 256, :].astype(BF)

    pl.semaphore_wait(barrier, len(peers))
    send_b = remote(bst, ops.at[0, c], pair_send.at[0], ag_recv.at[0], partner)
    send_b.start()
    send_w = remote(wts.at[c], wts.at[c], pair_send.at[1], pair_recv.at[0], partner)
    send_w.start()

    def gather(send):
        axis, r1, v, r = send
        to, dev = (STEP[r, 0, v], first(r)) if axis == 1 else (STEP[r1, r, v], second(r))
        return remote(ops.at[STEP[r1, 0, v]], ops.at[to], ag_send.at[ALL_SENDS.index(send)], ag_recv.at[to], dev)

    def arrived(i):
        remote(ops.at[i], ops.at[i], ag_send.at[0], ag_recv.at[i], partner).wait_recv()

    def send_r(i, core):
        part = pl.ds(pl.multiple_of(core * 1024 + i * 256, 256), 256)
        return remote(res.at[part], res.at[part], res_send.at[i], res_recv.at[i], partner)

    def ag_y(core, n):
        return remote(ops.at[0, core], ops.at[3, core], ag_send.at[30 + n], ag_recv.at[3 + 32 * n], y_near)

    def near(r, core, n):
        to = STEP[r, 0, 0]
        return remote(ops.at[0, core], ops.at[to, core], ag_send.at[32 + r // 2 + 2 * n],
                      ag_recv.at[to + 32 * n], first(r))

    ag_y(c, 0).start()
    for r in (1, 3):
        near(r, c, 0).start()
    for i in range(4):
        send_r(i, c).start()
    remote(bst, ops.at[0, 1 - c], pair_send.at[0], ag_recv.at[0], partner).wait_recv()
    ag_y(1 - c, 1).start()
    for r in (1, 3):
        near(r, 1 - c, 1).start()

    remote(wts.at[1 - c], wts.at[1 - c], pair_send.at[1], pair_recv.at[0], partner).wait_recv()
    for i in range(4):
        send_r(i, 1 - c).wait_recv()

    def exchange(i):
        return remote(give.at[i], take.at[i], ex_send.at[i], ex_recv.at[i], y_far)

    def put_partner(i, rows):
        return remote(done.at[i], out.at[:, rows, :], fin_send.at[i], fin_recv.at[i], partner)

    @pl.loop(0, STEPS + LAG)
    def _(i):
        @pl.when(i < STEPS)
        def _():
            @pl.when(i > 3)
            def _():
                arrived(i)

            for r in (1, 3):
                @pl.when(i == STEP[r, 0, 0])
                def _():
                    near(r, c, 0).wait_recv()
                    near(r, 1 - c, 1).wait_recv()

            @pl.when(i == 3)
            def _():
                ag_y(c, 0).wait_recv()
                ag_y(1 - c, 1).wait_recv()

            for step, sends in SENDS.items():
                @pl.when(i == step)
                def _():
                    for send in sends:
                        gather(send).start()

            for s in range(2):
                for half in range(2):
                    lanes = [slice(half * 512 + n * 128, half * 512 + (n + 1) * 128) for n in range(4)]
                    b = [[ops[i, s, k, :, lane].astype(F32) for lane in lanes] for k in range(4)]
                    for t in range(6):
                        w = [jnp.broadcast_to(wts[s, t * 4 + k:t * 4 + k + 1, :], (16, 128)) for k in range(4)]
                        for n in range(4):
                            acc = (b[0][n] * w[0] + b[1][n] * w[1]) + (b[2][n] * w[2] + b[3][n] * w[3])
                            col = s * 1024 + half * 512 + n * 128
                            wide[t * 16:t * 16 + 16, col:col + 128] = acc.astype(BF)
            for n in range(4):
                cols = slice(n * 256, (n + 1) * 256)
                part = jnp.dot(wide[...], res[:, cols], preferred_element_type=F32)
                give[i, :, cols] = part[:48].astype(BF)
                own[i, :, cols] = part[48:]
            exchange(i).start()

        @pl.when(i >= LAG)
        def _():
            w = i - LAG
            exchange(w).wait_recv()
            firsts = [own[w, t * 16:t * 16 + 16, :] + take[w, t * 16:t * 16 + 16, :].astype(F32) for t in range(2)]
            extra = own[w, 32:48, :] + take[w, 32:48, :].astype(F32)
            mask = [jnp.broadcast_to(wts[c, 24 + t:25 + t, 0:1], (16, 1)) for t in range(2)]
            even = lax.rem(c + 1, 2).astype(F32)
            odd = c.astype(F32)
            done[w, 0] = (firsts[0] * odd + firsts[1] * even)
            done[w, 1] = (extra * (mask[0] * odd + mask[1] * even))
            rows = rows_of(w, c)
            put_partner(w, rows).start()
            out[0, rows, :] = (firsts[0] * even + firsts[1] * odd)
            out[1, rows, :] = (extra * (mask[0] * even + mask[1] * odd))

    send_b.wait_send()
    send_w.wait_send()
    ag_y(c, 0).wait_send()
    ag_y(1 - c, 1).wait_send()
    for i in range(4):
        send_r(i, c).wait_send()
    for send in ALL_SENDS[len(FIRST_SENDS):]:
        gather(send).wait_send()
    for r in (1, 3):
        near(r, c, 0).wait_send()
        near(r, 1 - c, 1).wait_send()

    @pl.loop(0, STEPS)
    def _(i):
        exchange(i).wait_send()

    for i in range(STEPS):
        put_partner(i, rows_of(i, c)).wait_send()
        put_partner(i, rows_of(i, 1 - c)).wait_recv()


def shards(broadcast_ops, resident_ops, integrals, owner_list):
    hbm = pl.BlockSpec(memory_space=pltpu.HBM)
    dma = pltpu.SemaphoreType.DMA
    result = pl.pallas_call(
        kernel,
        out_shape=OUT,
        in_specs=[hbm, hbm, hbm, hbm],
        out_specs=pl.BlockSpec(memory_space=pltpu.VMEM),
        scratch_shapes=[
            pltpu.VMEM((4, 32, 1024), F32),
            pltpu.VMEM((1024, 1024), F32),
            pltpu.VMEM((4, 16, 1024), BF),
            pltpu.VMEM((STEPS, 2, 4, 16, 1024), BF),
            pltpu.VMEM((2048, 1024), BF),
            pltpu.SMEM((4, 4), F32),
            pltpu.SMEM((4,), jnp.int32),
            pltpu.VMEM((2, 32, 128), F32),
            pltpu.VMEM((96, 2048), BF),
            pltpu.VMEM((STEPS, 48, 1024), BF),
            pltpu.VMEM((STEPS, 48, 1024), BF),
            pltpu.VMEM((STEPS, 48, 1024), F32),
            pltpu.VMEM((STEPS, 2, 16, 1024), F32),
            dma((7,)), dma((2,)), dma((1,)), dma((4,)), dma((4,)), dma((36,)), dma((STEPS + 4,)), dma((STEPS,)),
            dma((STEPS,)), dma((STEPS,)), dma((STEPS,)),
        ],
        compiler_params=pltpu.CompilerParams(
            collective_id=0, has_side_effects=True, vmem_limit_bytes=67043328 - 8388608
        ),
    )(broadcast_ops[0], resident_ops[0, 0], integrals[0, 0], owner_list[0])
    return result[None, None]


OUT = pltpu.VMEM((2, 1024, 1024), F32)


def solution(mesh):
    in_specs = (
        P("sector", None, "owner", None),
        P("sector", "owner", None, None),
        P("sector", "owner", None, None),
        P("owner", None),
    )
    out_specs = P("sector", "owner", None, None, None)
    return jax.shard_map(shards, mesh=mesh, in_specs=in_specs, out_specs=out_specs, check_vma=False)
```
